32 devices in a mesh: dp: 8 (over z, core), ctx: 4 (over y, x).
Axes of the slice: x: 2, y: 2, z: 4, core: 2. Of those that a mesh axis runs over, the one named last changes fastest.
Arguments:
- layer_input: bfloat16 [8, 640, 4096], P('dp', 'ctx'), may hold values from -6 to 6
- queries: bfloat16 [8, 640, 2048], P('dp', 'ctx'), may hold values from -6 to 6, as said below
- key_rows: bfloat16 [8, 640, 2048], P('dp', 'ctx'), may hold values from -6 to 6, as said below
- value_rows: bfloat16 [8, 640, 2048], P('dp', 'ctx'), may hold values from -6 to 6
- attn_out: bfloat16 [8, 640, 2048], P('dp', 'ctx'), may hold values from -3 to 3
- out_grad: bfloat16 [8, 640, 2048], P('dp', 'ctx'), may hold values from -0.15625 to 0.15625
- layer_grad: bfloat16 [8, 640, 4096], P('dp', 'ctx'), may hold values from -0.078125 to 0.078125
- logsum: float32 [8, 16, 640], P('dp'), may hold values from -12 to 16, as said below
- projector: bfloat16 [4096, 512], replicated, may hold values from -0.09375 to 0.09375
Outputs:
- weight_grads: float32 [4, 512, 2048], P(None, ('dp', 'ctx'))
The draws below stay inside these ranges and needn't reach their ends.
Inputs may be any that keep to these rules, and one draw needn't show every extreme that they name: `queries`: drawn together with key_rows and logsum. `key_rows`: drawn together with queries and logsum. logsum[s, h, t] is the logarithm of the sum over u <= t of exp(scores[s, h, t, u]), scores as in the reference program, from the bfloat16 queries and key_rows.
All inputs are finite; a program needn't handle non-finite values.
Results may differ from the reference program's by a relative error of at most 0.0033.
Values may be sent and summed in bfloat16 or wider, within the bound.
A program may use at most 320 MiB of HBM per device.

```python
import math
import jax
import jax.numpy as jnp
from jax import lax

D = 4096
HEADS = 16
HEAD_DIM = 128
RANK = 512
TOKENS = 640
SEQS = 8


def joint_draw(key):
    query_key = jax.random.fold_in(key, 101)
    other_key = jax.random.fold_in(key, 202)
    shape = (SEQS, TOKENS, HEADS * HEAD_DIM)
    first = jnp.clip(jax.random.normal(query_key, shape, jnp.float32), -6.0, 6.0)
    second = jnp.clip(jax.random.normal(other_key, shape, jnp.float32), -6.0, 6.0)
    return (first.astype(jnp.bfloat16), second.astype(jnp.bfloat16))


def draw_queries(key, part):
    return joint_draw(key)[0]


def draw_key_rows(key, part):
    return joint_draw(key)[1]


def draw_logsum(key, part):
    first, second = joint_draw(key)
    scaling = 1.0 / math.sqrt(HEAD_DIM)

    def one_sequence(members):
        query_seq, key_seq = members
        query3 = query_seq.astype(jnp.float32).reshape(TOKENS, HEADS, HEAD_DIM)
        key3 = key_seq.astype(jnp.float32).reshape(TOKENS, HEADS, HEAD_DIM)
        scores = jnp.einsum('thd,uhd->htu', query3, key3, precision=lax.Precision.HIGHEST) * scaling
        positions = lax.iota(jnp.int32, TOKENS)
        causal = positions[:, None] >= positions[None, :]
        masked = jnp.where(causal[None], scores, jnp.float32(-1e+30))
        return jax.scipy.special.logsumexp(masked, axis=-1)
    return lax.map(one_sequence, (first, second))


def levels(stream_key, dims, cuts, least, top_value):
    def one(dim, blocks):
        draws = jax.random.uniform(jax.random.fold_in(jax.random.fold_in(stream_key, 6), dim), (blocks,), jnp.float32, least / len(cuts), top_value / len(cuts))
        return jnp.repeat(jnp.exp(draws), dims[dim] // blocks).reshape((-1,) + (1,) * (len(dims) - dim - 1))

    gain = one(*cuts[0])
    for cut in cuts[1:]:
        gain = gain * one(*cut)
    return gain


def normal_values(own_key, extent, scale, bound, shards=(), dtype=jnp.bfloat16):
    factor_of = levels(own_key, extent, shards, -0.22, 0.18) if shards else 1.0
    entries = jax.random.normal(own_key, extent, jnp.float32) * scale * factor_of
    return jnp.minimum(jnp.maximum(entries, -bound), bound).astype(dtype)


def setup_inputs(seed: int = 0) -> dict:
    keys = jax.random.split(jax.random.key(seed), 10)
    return {
        "layer_input": normal_values(keys[0], (SEQS, TOKENS, D), 1.0, 6.0, ((0, 8), (1, 4))),
        "queries": draw_queries(jax.random.fold_in(keys[9], 71), 0),
        "key_rows": draw_key_rows(jax.random.fold_in(keys[9], 71), 0),
        "value_rows": normal_values(keys[3], (SEQS, TOKENS, HEADS * HEAD_DIM), 1.0, 6.0, ((0, 8), (1, 4))),
        "attn_out": normal_values(keys[4], (SEQS, TOKENS, HEADS * HEAD_DIM), 0.5, 3.0, ((0, 8), (1, 4))),
        "out_grad": normal_values(keys[5], (SEQS, TOKENS, HEADS * HEAD_DIM), (2.0 / (SEQS * TOKENS) ** 0.5), 0.15625, ((0, 8), (1, 4))),
        "layer_grad": normal_values(keys[6], (SEQS, TOKENS, D), (1.0 / (SEQS * TOKENS) ** 0.5), 0.078125, ((0, 8), (1, 4))),
        "logsum": draw_logsum(jax.random.fold_in(keys[9], 71), 0),
        "projector": normal_values(keys[8], (D, RANK), D ** -0.5, 0.09375),
    }


def reference(layer_input, queries, key_rows, value_rows, attn_out, out_grad, layer_grad, logsum, projector):
    scaling = 1.0 / math.sqrt(HEAD_DIM)
    feature_width = HEADS * HEAD_DIM
    highest = lax.Precision.HIGHEST

    def one_sequence(totals, members):
        input_seq, query_seq, key_seq, value_seq, out_seq, grad_seq, layer_seq, logsum_seq = members
        reduced_in = jnp.dot(input_seq, projector, preferred_element_type=jnp.float32).astype(jnp.bfloat16)
        reduced_grad = jnp.dot(layer_seq, projector, preferred_element_type=jnp.float32).astype(jnp.bfloat16)
        query3 = query_seq.astype(jnp.float32).reshape(TOKENS, HEADS, HEAD_DIM)
        key3 = key_seq.astype(jnp.float32).reshape(TOKENS, HEADS, HEAD_DIM)
        value3 = value_seq.astype(jnp.float32).reshape(TOKENS, HEADS, HEAD_DIM)
        grad3 = grad_seq.astype(jnp.float32).reshape(TOKENS, HEADS, HEAD_DIM)
        out3 = out_seq.astype(jnp.float32).reshape(TOKENS, HEADS, HEAD_DIM)
        scores = jnp.einsum('thd,uhd->htu', query3, key3, precision=highest) * scaling
        positions = lax.iota(jnp.int32, TOKENS)
        causal = positions[:, None] >= positions[None, :]
        prob = jnp.where(causal[None], jnp.exp(scores - logsum_seq[:, :, None]), jnp.float32(0.0))
        deltas = lax.optimization_barrier(jnp.sum(grad3 * out3, axis=-1)).T
        dprob = jnp.einsum('thd,uhd->htu', grad3, value3, precision=highest)
        dscore = prob * (dprob - deltas[:, :, None]) * scaling
        score_low = lax.optimization_barrier(dscore.astype(jnp.bfloat16)).astype(jnp.float32)
        prob_low = lax.optimization_barrier(prob.astype(jnp.bfloat16)).astype(jnp.float32)
        dquery = jnp.einsum('htu,uhd->thd', score_low, key3, precision=highest).reshape(TOKENS, feature_width)
        dkey = jnp.einsum('htu,thd->uhd', score_low, query3, precision=highest).reshape(TOKENS, feature_width)
        dvalue = jnp.einsum('htu,thd->uhd', prob_low, grad3, precision=highest).reshape(TOKENS, feature_width)
        widened = reduced_in.astype(jnp.float32)
        grad_query = jnp.dot(widened.T, dquery, precision=highest)
        grad_key = jnp.dot(widened.T, dkey, precision=highest)
        grad_value = jnp.dot(widened.T, dvalue, precision=highest)
        grad_output = jnp.dot(reduced_grad.T, out_seq, preferred_element_type=jnp.float32)
        return (totals + jnp.stack([grad_query, grad_key, grad_value, grad_output]), None)
    initial = jnp.zeros((4, RANK, feature_width), jnp.float32)
    result, unused = lax.scan(one_sequence, initial, (layer_input, queries, key_rows, value_rows, attn_out, out_grad, layer_grad, logsum))
    return result
```

```python
import functools
import math

import jax
import jax.numpy as jnp
from jax import lax
from jax.experimental import pallas as pl
from jax.experimental.pallas import tpu as pltpu
from jax.sharding import PartitionSpec as P

BLOCK = 128


def dot(left, right, dims):
    return lax.dot_general(left, right, (dims, ((), ())), preferred_element_type=jnp.float32)


def head_kernel(
    q_ref, k_ref, v_ref, g_ref, o_ref, sums_ref, rin_ref, rgrad_ref, out_ref, rin_t, rgrad_t, acc
):
    tokens, width = q_ref.shape
    scaling = 1.0 / math.sqrt(width)

    @pl.when(pl.program_id(0) == 0)
    def _():
        rin_t[...] = rin_ref[...].T
        rgrad_t[...] = rgrad_ref[...].T

    product = g_ref[...].astype(jnp.float32) * o_ref[...].astype(jnp.float32)
    deltas = jnp.sum(product.T, axis=0, keepdims=True)
    sums = sums_ref[0]
    row = lax.broadcasted_iota(jnp.int32, (BLOCK, BLOCK), 0)
    col = lax.broadcasted_iota(jnp.int32, (BLOCK, BLOCK), 1)
    causal = row <= col
    for start in range(0, tokens, BLOCK):
        keys = k_ref[start : start + BLOCK]
        values = v_ref[start : start + BLOCK]
        queries = q_ref[start:]
        grads = g_ref[start:]
        scores = dot(keys, queries, ((1,), (1,))) * scaling
        prob = jnp.exp(scores - sums[:, start:])
        diagonal = jnp.where(causal, prob[:, :BLOCK], 0.0)
        if start + BLOCK < tokens:
            prob = jnp.concatenate([diagonal, prob[:, BLOCK:]], axis=1)
        else:
            prob = diagonal
        dprob = dot(values, grads, ((1,), (1,)))
        dscore = prob * (dprob - deltas[:, start:]) * scaling
        score_low = dscore.astype(jnp.bfloat16)
        prob_low = prob.astype(jnp.bfloat16)
        dquery = dot(score_low, keys, ((0,), (0,)))
        if start == 0:
            acc[:, :width] = dquery
        else:
            acc[start:, :width] += dquery
        acc[start : start + BLOCK, width : 2 * width] = dot(score_low, queries, ((1,), (0,)))
        acc[start : start + BLOCK, 2 * width :] = dot(prob_low, grads, ((1,), (0,)))
    full = acc[...]
    upper = full.astype(jnp.bfloat16)
    lower = (full - upper.astype(jnp.float32)).astype(jnp.bfloat16)
    joined = dot(rin_t[...], upper, ((1,), (0,))) + dot(rin_t[...], lower, ((1,), (0,)))
    for index in range(3):
        out_ref[index] = joined[:, index * width : (index + 1) * width].astype(out_ref.dtype)
    out_ref[3] = dot(rgrad_t[...], o_ref[...], ((1,), (0,))).astype(out_ref.dtype)


def head_grads(q, k, v, g, o, sums, rin, rgrad):
    tokens, columns = q.shape
    heads = sums.shape[0]
    width = columns // heads
    rank = rin.shape[1]
    rows = pl.BlockSpec((tokens, width), lambda h: (0, h))
    whole = pl.BlockSpec((tokens, rank), lambda h: (0, 0))
    return pl.pallas_call(
        head_kernel,
        grid=(heads,),
        out_shape=jax.ShapeDtypeStruct((4, rank, columns), jnp.bfloat16),
        in_specs=[rows] * 5 + [pl.BlockSpec((1, 1, tokens), lambda h: (h, 0, 0)), whole, whole],
        out_specs=pl.BlockSpec((4, rank, width), lambda h: (0, 0, h)),
        scratch_shapes=[
            pltpu.VMEM((rank, tokens), jnp.bfloat16),
            pltpu.VMEM((rank, tokens), jnp.bfloat16),
            pltpu.VMEM((tokens, 3 * width), jnp.float32),
        ],
        compiler_params=pltpu.CompilerParams(vmem_limit_bytes=48 * 1024 * 1024),
    )(q, k, v, g, o, sums, rin, rgrad)


def on_device(
    dp_size,
    ctx_size,
    layer_input,
    queries,
    key_rows,
    value_rows,
    attn_out,
    out_grad,
    layer_grad,
    logsum,
    projector,
):
    heads = logsum.shape[1] // ctx_size
    reduced_in = jnp.dot(layer_input[0], projector, preferred_element_type=jnp.float32)
    reduced_grad = jnp.dot(layer_grad[0], projector, preferred_element_type=jnp.float32)
    reduced_in = reduced_in.astype(jnp.bfloat16)
    reduced_grad = reduced_grad.astype(jnp.bfloat16)

    def by_heads(rows):
        return lax.all_to_all(rows[0], "ctx", split_axis=1, concat_axis=0, tiled=True)

    q, k, v, g, o = map(by_heads, (queries, key_rows, value_rows, out_grad, attn_out))
    rin = lax.all_gather(reduced_in, "ctx", axis=0, tiled=True)
    rgrad = lax.all_gather(reduced_grad, "ctx", axis=0, tiled=True)
    sums = lax.dynamic_slice_in_dim(logsum[0], lax.axis_index("ctx") * heads, heads, 0)
    partial = head_grads(q, k, v, g, o, sums[:, None], rin, rgrad)
    count, rank, columns = partial.shape
    pieces = partial.reshape(count, dp_size, rank // dp_size, columns)
    pieces = lax.all_to_all(pieces, "dp", split_axis=1, concat_axis=1, tiled=True)
    summed = jnp.sum(pieces.astype(jnp.float32), axis=1)
    return lax.all_to_all(summed, "ctx", split_axis=1, concat_axis=2, tiled=True)


def solution(mesh):
    rows = P("dp", "ctx", None)
    placed = (rows,) * 7 + (P("dp", None, None), P())
    return jax.shard_map(
        functools.partial(on_device, mesh.shape["dp"], mesh.shape["ctx"]),
        mesh=mesh,
        in_specs=placed,
        out_specs=P(None, ("dp", "ctx"), None),
        check_vma=False,
    )
```

```python
import functools
import math

import jax
import jax.numpy as jnp
from jax import lax
from jax.experimental import pallas as pl
from jax.experimental.pallas import tpu as pltpu
from jax.sharding import PartitionSpec as P

BLOCK = 128
DEPTH = 512
MESH = pl.DeviceIdType.MESH


def dot(left, right, dims):
    return lax.dot_general(left, right, (dims, ((), ())), preferred_element_type=jnp.float32)


def head_products(arrays, head, sums, acc):
    q_ref, k_ref, v_ref, g_ref, o_ref = (arrays.at[index, head] for index in range(5))
    tokens, width = q_ref.shape
    scaling = 1.0 / math.sqrt(width)
    product = g_ref[...].astype(jnp.float32) * o_ref[...].astype(jnp.float32)
    deltas = jnp.sum(product.T, axis=0, keepdims=True)
    row = lax.broadcasted_iota(jnp.int32, (BLOCK, BLOCK), 0)
    col = lax.broadcasted_iota(jnp.int32, (BLOCK, BLOCK), 1)
    causal = row <= col
    for start in range(0, tokens, BLOCK):
        keys = k_ref[start : start + BLOCK]
        values = v_ref[start : start + BLOCK]
        queries = q_ref[start:]
        grads = g_ref[start:]
        scores = dot(keys, queries, ((1,), (1,))) * scaling
        prob = jnp.exp(scores - sums[:, start:])
        diagonal = jnp.where(causal, prob[:, :BLOCK], 0.0)
        if start + BLOCK < tokens:
            prob = jnp.concatenate([diagonal, prob[:, BLOCK:]], axis=1)
        else:
            prob = diagonal
        dprob = dot(values, grads, ((1,), (1,)))
        dscore = prob * (dprob - deltas[:, start:]) * scaling
        score_low = dscore.astype(jnp.bfloat16)
        prob_low = prob.astype(jnp.bfloat16)
        dquery = dot(score_low, keys, ((0,), (0,)))
        if start == 0:
            acc[:, :width] = dquery
        else:
            acc[start:, :width] += dquery
        acc[start : start + BLOCK, width : 2 * width] = dot(score_low, queries, ((1,), (0,)))
        acc[start : start + BLOCK, 2 * width :] = dot(prob_low, grads, ((1,), (0,)))


def kernel(
    dp_size,
    ctx_size,
    layer_input,
    q_hbm,
    k_hbm,
    v_hbm,
    o_hbm,
    g_hbm,
    layer_grad,
    sums_ref,
    projector,
    out_ref,
    arrays,
    rows_in,
    proj,
    proj_acc,
    reduced,
    reduced_t,
    acc,
    own,
    pair_out,
    pair_in,
    z_out,
    z_in,
    final_out,
    final_in,
    load_sem,
    local_sem,
    head_send,
    head_recv,
    red_send,
    red_recv,
    pair_send,
    pair_recv,
    z_send,
    z_recv,
    final_send,
    final_recv,
):
    me = lax.axis_index("ctx")
    place = lax.axis_index("dp")
    core = place % 2
    level = place // 2
    levels = dp_size // 2
    partner = place + 1 - 2 * core
    sources = (q_hbm, k_hbm, v_hbm, g_hbm, o_hbm)
    heads = arrays.shape[1]
    rows = q_hbm.shape[0]
    width = arrays.shape[3]
    depth = projector.shape[0]
    piece = own.shape[4]
    slab = final_out.shape[3]
    mine = pl.ds(pl.multiple_of(me * rows, 16), rows)

    def ctx_peer(d):
        return lax.rem(me + d, ctx_size)

    def columns(owner, head):
        return pl.ds(pl.multiple_of((owner * heads + head) * width, width), width)

    def remote(src, dst, send, recv, **where):
        return pltpu.make_async_remote_copy(
            src_ref=src,
            dst_ref=dst,
            send_sem=send,
            recv_sem=recv,
            device_id=where,
            device_id_type=MESH,
        )

    def local_copy(head, index):
        return pltpu.make_async_copy(
            sources[index].at[:, columns(me, head)],
            arrays.at[index, head, mine],
            local_sem.at[head, index],
        )

    def head_copy(head, index, d):
        peer = ctx_peer(d)
        return remote(
            sources[index].at[:, columns(peer, head)],
            arrays.at[index, head, mine],
            head_send.at[head, index, d - 1],
            head_recv.at[head, index, d - 1],
            ctx=peer,
        )

    def reduced_copy(which, d):
        return remote(
            reduced.at[which, mine],
            reduced.at[which, mine],
            red_send.at[which, d - 1],
            red_recv.at[which, d - 1],
            ctx=ctx_peer(d),
        )

    def pair_copy(head):
        return remote(
            pair_out.at[head],
            pair_in.at[head],
            pair_send.at[head],
            pair_recv.at[head],
            dp=partner,
        )

    def z_copy(head, d):
        peer = lax.rem(level + d, levels)
        return remote(
            z_out.at[head, peer],
            z_in.at[head, d - 1],
            z_send.at[head, d - 1],
            z_recv.at[head, d - 1],
            dp=peer * 2 + core,
        )

    def final_copy(head, d):
        peer = ctx_peer(d)
        return remote(
            final_out.at[head, peer],
            final_in.at[head, d - 1],
            final_send.at[head, d - 1],
            final_recv.at[head, d - 1],
            ctx=peer,
        )

    def start_head(head):
        for index in range(5):
            for d in range(1, ctx_size):
                head_copy(head, index, d).start()
        for index in range(5):
            local_copy(head, index).start()

    loads = (
        pltpu.make_async_copy(projector, proj, load_sem.at[0]),
        pltpu.make_async_copy(layer_input, rows_in.at[:rows], load_sem.at[1]),
        pltpu.make_async_copy(layer_grad, rows_in.at[rows:], load_sem.at[2]),
    )
    for load in loads:
        load.start()
    barrier = pltpu.get_barrier_semaphore()
    for d in range(1, ctx_size):
        pl.semaphore_signal(barrier, inc=1, device_id={"ctx": ctx_peer(d)}, device_id_type=MESH)
    pl.semaphore_signal(barrier, inc=1, device_id={"dp": partner}, device_id_type=MESH)
    for d in range(1, levels):
        peer = lax.rem(level + d, levels) * 2 + core
        pl.semaphore_signal(barrier, inc=1, device_id={"dp": peer}, device_id_type=MESH)
    pl.semaphore_wait(barrier, ctx_size + levels - 1)

    start_head(0)
    for load in loads:
        load.wait()
    proj_acc[...] = jnp.zeros_like(proj_acc)

    @pl.loop(0, depth // DEPTH)
    def _(step):
        at = pl.ds(pl.multiple_of(step * DEPTH, DEPTH), DEPTH)
        proj_acc[...] += dot(rows_in[:, at], proj[at], ((1,), (0,)))

    for which in range(2):
        reduced[which, mine] = proj_acc[which * rows : (which + 1) * rows].astype(jnp.bfloat16)
        for d in range(1, ctx_size):
            reduced_copy(which, d).start()

    @pl.loop(1, heads)
    def _(head):
        start_head(head)

    def compute(head):
        for index in range(5):
            local_copy(head, index).wait()
            for d in range(1, ctx_size):
                head_copy(head, index, d).wait_recv()
        sums = sums_ref[pl.ds(me * heads + head, 1), :]
        head_products(arrays, head, sums, acc)

        @pl.when(head == 0)
        def _():
            for which in range(2):
                for d in range(1, ctx_size):
                    reduced_copy(which, d).wait_recv()
                reduced_t[which] = reduced[which].T

        full = acc[...]
        upper = full.astype(jnp.bfloat16)
        lower = (full - upper.astype(jnp.float32)).astype(jnp.bfloat16)
        left = reduced_t[0]
        joined = dot(left, upper, ((1,), (0,))) + dot(left, lower, ((1,), (0,)))
        last = dot(reduced_t[1], arrays[4, head], ((1,), (0,)))
        for part in range(dp_size):
            span = slice(part * piece, (part + 1) * piece)
            for index in range(3):
                own[head, part // 2, part % 2, index] = joined[
                    span, index * width : (index + 1) * width
                ]
            own[head, part // 2, part % 2, 3] = last[span]
        for to in range(levels):
            pair_out[head, to] = own[head, to, 1 - core].astype(pair_out.dtype)
        pair_copy(head).start()

    def add_pair(head):
        pair_copy(head).wait_recv()
        for to in range(levels):
            total = own[head, to, core] + pair_in[head, to].astype(jnp.float32)
            own[head, to, core] = total
            z_out[head, to] = total.astype(z_out.dtype)
        for d in range(1, levels):
            z_copy(head, d).start()

    def add_levels(head):
        total = own[head, level, core]
        for d in range(1, levels):
            z_copy(head, d).wait_recv()
            total += z_in[head, d - 1].astype(jnp.float32)
        for to in range(ctx_size):
            final_out[head, to] = total[:, to * slab : (to + 1) * slab]
        for d in range(1, ctx_size):
            final_copy(head, d).start()

    @pl.loop(0, heads + 2)
    def _(step):
        @pl.when(step < heads)
        def _():
            compute(step)

        @pl.when(jnp.logical_and(step >= 1, step < heads + 1))
        def _():
            add_pair(step - 1)

        @pl.when(step >= 2)
        def _():
            add_levels(step - 2)

    @pl.loop(0, heads)
    def _(head):
        out_ref[:, :, columns(me, head)] = final_out[head, me]
        for d in range(1, ctx_size):
            final_copy(head, d).wait()
            owner = lax.rem(me + ctx_size - d, ctx_size)
            out_ref[:, :, columns(owner, head)] = final_in[head, d - 1]
        pair_copy(head).wait_send()
        for d in range(1, levels):
            z_copy(head, d).wait_send()
        for index in range(5):
            for d in range(1, ctx_size):
                head_copy(head, index, d).wait_send()

    for which in range(2):
        for d in range(1, ctx_size):
            reduced_copy(which, d).wait_send()


def on_device(
    dp_size,
    ctx_size,
    layer_input,
    queries,
    key_rows,
    value_rows,
    attn_out,
    out_grad,
    layer_grad,
    logsum,
    projector,
):
    rows, features = queries.shape[1:]
    all_heads, tokens = logsum.shape[1:]
    heads = all_heads // ctx_size
    width = features // all_heads
    depth, rank = projector.shape
    levels = dp_size // 2
    piece = rank // dp_size
    slab = piece // ctx_size
    low, wide = jnp.bfloat16, jnp.float32
    dma = pltpu.SemaphoreType.DMA
    anywhere = pl.BlockSpec(memory_space=pl.ANY)
    in_vmem = pl.BlockSpec(memory_space=pltpu.VMEM)
    return pl.pallas_call(
        functools.partial(kernel, dp_size, ctx_size),
        out_shape=jax.ShapeDtypeStruct((4, slab, features), wide),
        in_specs=[anywhere] * 7 + [in_vmem, anywhere],
        out_specs=in_vmem,
        scratch_shapes=[
            pltpu.VMEM((5, heads, tokens, width), low),
            pltpu.VMEM((2 * rows, depth), low),
            pltpu.VMEM((depth, rank), low),
            pltpu.VMEM((2 * rows, rank), wide),
            pltpu.VMEM((2, tokens, rank), low),
            pltpu.VMEM((2, rank, tokens), low),
            pltpu.VMEM((tokens, 3 * width), wide),
            pltpu.VMEM((heads, levels, 2, 4, piece, width), wide),
            pltpu.VMEM((heads, levels, 4, piece, width), low),
            pltpu.VMEM((heads, levels, 4, piece, width), low),
            pltpu.VMEM((heads, levels, 4, piece, width), low),
            pltpu.VMEM((heads, levels - 1, 4, piece, width), low),
            pltpu.VMEM((heads, ctx_size, 4, slab, width), wide),
            pltpu.VMEM((heads, ctx_size - 1, 4, slab, width), wide),
            dma((3,)),
            dma((heads, 5)),
            dma((heads, 5, ctx_size - 1)),
            dma((heads, 5, ctx_size - 1)),
            dma((2, ctx_size - 1)),
            dma((2, ctx_size - 1)),
            dma((heads,)),
            dma((heads,)),
            dma((heads, levels - 1)),
            dma((heads, levels - 1)),
            dma((heads, ctx_size - 1)),
            dma((heads, ctx_size - 1)),
        ],
        compiler_params=pltpu.CompilerParams(
            collective_id=0, has_side_effects=True, vmem_limit_bytes=56 * 1024 * 1024
        ),
    )(
        layer_input[0],
        queries[0],
        key_rows[0],
        value_rows[0],
        attn_out[0],
        out_grad[0],
        layer_grad[0],
        logsum[0],
        projector,
    )


def solution(mesh):
    rows = P("dp", "ctx", None)
    placed = (rows,) * 7 + (P("dp", None, None), P())
    return jax.shard_map(
        functools.partial(on_device, mesh.shape["dp"], mesh.shape["ctx"]),
        mesh=mesh,
        in_specs=placed,
        out_specs=P(None, ("dp", "ctx"), None),
        check_vma=False,
    )
```

```python
import functools
import math

import jax
import jax.numpy as jnp
from jax import lax
from jax.experimental import pallas as pl
from jax.experimental.pallas import tpu as pltpu
from jax.sharding import PartitionSpec as P

BLOCK = 128
DEPTH = 512
MESH = pl.DeviceIdType.MESH


def dot(left, right, dims):
    return lax.dot_general(left, right, (dims, ((), ())), preferred_element_type=jnp.float32)


def head_products(arrays, head, sums, deltas, acc):
    q_ref, k_ref, v_ref, g_ref = (arrays.at[index, head] for index in range(4))
    tokens, width = q_ref.shape
    scaling = 1.0 / math.sqrt(width)
    row = lax.broadcasted_iota(jnp.int32, (BLOCK, BLOCK), 0)
    col = lax.broadcasted_iota(jnp.int32, (BLOCK, BLOCK), 1)
    causal = row <= col
    for start in range(0, tokens, BLOCK):
        keys = k_ref[start : start + BLOCK]
        values = v_ref[start : start + BLOCK]
        queries = q_ref[start:]
        grads = g_ref[start:]
        scores = dot(keys, queries, ((1,), (1,))) * scaling
        prob = jnp.exp(scores - sums[:, start:])
        diagonal = jnp.where(causal, prob[:, :BLOCK], 0.0)
        if start + BLOCK < tokens:
            prob = jnp.concatenate([diagonal, prob[:, BLOCK:]], axis=1)
        else:
            prob = diagonal
        dprob = dot(values, grads, ((1,), (1,)))
        dscore = prob * (dprob - deltas[:, start:]) * scaling
        score_low = dscore.astype(jnp.bfloat16)
        prob_low = prob.astype(jnp.bfloat16)
        dquery = dot(score_low, keys, ((0,), (0,)))
        if start == 0:
            acc[:, :width] = dquery
        else:
            acc[start:, :width] += dquery
        acc[start : start + BLOCK, width : 2 * width] = dot(score_low, queries, ((1,), (0,)))
        acc[start : start + BLOCK, 2 * width :] = dot(prob_low, grads, ((1,), (0,)))


def kernel(
    dp_size,
    ctx_size,
    layer_input,
    q_hbm,
    k_hbm,
    v_hbm,
    o_hbm,
    g_hbm,
    layer_grad,
    sums_ref,
    projector,
    out_ref,
    arrays,
    rows_in,
    proj,
    proj_acc,
    grad_own,
    out_own,
    reduced,
    reduced_t,
    reduced_grad,
    delta_out,
    delta_in,
    delta_rows,
    acc,
    own,
    pair_out,
    pair_in,
    z_out,
    z_in,
    final_out,
    final_in,
    own_o,
    pair_out_o,
    pair_in_o,
    z_out_o,
    z_in_o,
    final_own_o,
    final_out_o,
    final_in_o,
    load_sem,
    local_sem,
    head_send,
    head_recv,
    red_send,
    red_recv,
    delta_send,
    delta_recv,
    pair_send,
    pair_recv,
    z_send,
    z_recv,
    final_send,
    final_recv,
    pair_send_o,
    pair_recv_o,
    z_send_o,
    z_recv_o,
    final_send_o,
    final_recv_o,
):
    me = lax.axis_index("ctx")
    place = lax.axis_index("dp")
    core = place % 2
    level = place // 2
    levels = dp_size // 2
    partner = place + 1 - 2 * core
    sources = (q_hbm, k_hbm, v_hbm, g_hbm)
    count = len(sources)
    heads = arrays.shape[1]
    rows = q_hbm.shape[0]
    width = arrays.shape[3]
    depth = projector.shape[0]
    piece = own.shape[4]
    slab = final_out.shape[3]
    mine = pl.ds(pl.multiple_of(me * rows, 16), rows)

    def ctx_peer(d):
        return lax.rem(me + d, ctx_size)

    def columns(owner, head):
        return pl.ds(pl.multiple_of((owner * heads + head) * width, width), width)

    def remote(src, dst, send, recv, **where):
        return pltpu.make_async_remote_copy(
            src_ref=src,
            dst_ref=dst,
            send_sem=send,
            recv_sem=recv,
            device_id=where,
            device_id_type=MESH,
        )

    def local_copy(head, index):
        return pltpu.make_async_copy(
            sources[index].at[:, columns(me, head)],
            arrays.at[index, head, mine],
            local_sem.at[head, index],
        )

    def head_copy(head, index, d):
        peer = ctx_peer(d)
        return remote(
            sources[index].at[:, columns(peer, head)],
            arrays.at[index, head, mine],
            head_send.at[head, index, d - 1],
            head_recv.at[head, index, d - 1],
            ctx=peer,
        )

    def reduced_copy(d):
        return remote(
            reduced.at[mine],
            reduced.at[mine],
            red_send.at[d - 1],
            red_recv.at[d - 1],
            ctx=ctx_peer(d),
        )

    def delta_copy(d):
        peer = ctx_peer(d)
        return remote(
            delta_out.at[peer],
            delta_in.at[me],
            delta_send.at[d - 1],
            delta_recv.at[d - 1],
            ctx=peer,
        )

    def pair_copy_o():
        return remote(pair_out_o, pair_in_o, pair_send_o, pair_recv_o, dp=partner)

    def z_copy_o(d):
        peer = lax.rem(level + d, levels)
        return remote(
            z_out_o.at[peer],
            z_in_o.at[d - 1],
            z_send_o.at[d - 1],
            z_recv_o.at[d - 1],
            dp=peer * 2 + core,
        )

    def final_copy_o(d):
        peer = ctx_peer(d)
        return remote(
            final_out_o.at[peer],
            final_in_o.at[d - 1],
            final_send_o.at[d - 1],
            final_recv_o.at[d - 1],
            ctx=peer,
        )

    def pair_copy(head):
        return remote(
            pair_out.at[head],
            pair_in.at[head],
            pair_send.at[head],
            pair_recv.at[head],
            dp=partner,
        )

    def z_copy(head, d):
        peer = lax.rem(level + d, levels)
        return remote(
            z_out.at[head, peer],
            z_in.at[head, d - 1],
            z_send.at[head, d - 1],
            z_recv.at[head, d - 1],
            dp=peer * 2 + core,
        )

    def final_copy(head, d):
        peer = ctx_peer(d)
        return remote(
            final_out.at[head, peer],
            final_in.at[head, d - 1],
            final_send.at[head, d - 1],
            final_recv.at[head, d - 1],
            ctx=peer,
        )

    def start_head(head):
        for index in range(count):
            for d in range(1, ctx_size):
                head_copy(head, index, d).start()
        for index in range(count):
            local_copy(head, index).start()

    loads = (
        pltpu.make_async_copy(projector, proj, load_sem.at[0]),
        pltpu.make_async_copy(layer_input, rows_in.at[:rows], load_sem.at[1]),
        pltpu.make_async_copy(layer_grad, rows_in.at[rows:], load_sem.at[2]),
        pltpu.make_async_copy(g_hbm, grad_own, load_sem.at[3]),
        pltpu.make_async_copy(o_hbm, out_own, load_sem.at[4]),
    )
    for load in loads:
        load.start()
    barrier = pltpu.get_barrier_semaphore()
    for d in range(1, ctx_size):
        pl.semaphore_signal(barrier, inc=1, device_id={"ctx": ctx_peer(d)}, device_id_type=MESH)
    pl.semaphore_signal(barrier, inc=1, device_id={"dp": partner}, device_id_type=MESH)
    for d in range(1, levels):
        peer = lax.rem(level + d, levels) * 2 + core
        pl.semaphore_signal(barrier, inc=1, device_id={"dp": peer}, device_id_type=MESH)
    pl.semaphore_wait(barrier, ctx_size + levels - 1)

    start_head(0)
    for load in loads:
        load.wait()
    proj_acc[...] = jnp.zeros_like(proj_acc)

    @pl.loop(0, depth // DEPTH)
    def _(step):
        at = pl.ds(pl.multiple_of(step * DEPTH, DEPTH), DEPTH)
        proj_acc[...] += dot(rows_in[:, at], proj[at], ((1,), (0,)))

    reduced[mine] = proj_acc[:rows].astype(jnp.bfloat16)
    for d in range(1, ctx_size):
        reduced_copy(d).start()
    reduced_grad[...] = proj_acc[rows:].astype(jnp.bfloat16)
    lane = lax.broadcasted_iota(jnp.int32, (rows, BLOCK), 1)
    table = jnp.zeros((rows, BLOCK), jnp.float32)
    for head in range(heads * ctx_size):
        span = slice(head * width, (head + 1) * width)
        product = grad_own[:, span].astype(jnp.float32) * out_own[:, span].astype(jnp.float32)
        table = jnp.where(lane == head, jnp.sum(product, axis=1, keepdims=True), table)
    table = table.T
    delta_out[...] = jnp.zeros_like(delta_out)
    for owner in range(ctx_size):
        delta_out[owner, :heads] = table[owner * heads : (owner + 1) * heads]
    delta_in[me] = delta_out[me]
    for d in range(1, ctx_size):
        delta_copy(d).start()

    @pl.loop(1, heads)
    def _(head):
        start_head(head)

    rgrad_t = reduced_grad[...].T
    for part in range(dp_size):
        span = slice(part * piece, (part + 1) * piece)
        own_o[part // 2, part % 2] = dot(rgrad_t[span], out_own[...], ((1,), (0,)))
    for to in range(levels):
        pair_out_o[to] = own_o[to, 1 - core].astype(pair_out_o.dtype)
    pair_copy_o().start()

    for d in range(1, ctx_size):
        delta_copy(d).wait_recv()
    delta_rows[...] = jnp.concatenate([delta_in[owner] for owner in range(ctx_size)], axis=1)

    pair_copy_o().wait_recv()
    for to in range(levels):
        total_o = own_o[to, core] + pair_in_o[to].astype(jnp.float32)
        own_o[to, core] = total_o
        z_out_o[to] = total_o.astype(z_out_o.dtype)
    for d in range(1, levels):
        z_copy_o(d).start()

    def add_levels_o():
        total = own_o[level, core]
        for d in range(1, levels):
            z_copy_o(d).wait_recv()
            total += z_in_o[d - 1].astype(jnp.float32)
        for to in range(ctx_size):
            part = total[to * slab : (to + 1) * slab]
            final_own_o[to] = part
            final_out_o[to] = part.astype(final_out_o.dtype)
        for d in range(1, ctx_size):
            final_copy_o(d).start()

    def compute(head):
        for index in range(count):
            local_copy(head, index).wait()
            for d in range(1, ctx_size):
                head_copy(head, index, d).wait_recv()
        sums = sums_ref[pl.ds(me * heads + head, 1), :]
        head_products(arrays, head, sums, delta_rows[pl.ds(head, 1), :], acc)

        @pl.when(head == 0)
        def _():
            for d in range(1, ctx_size):
                reduced_copy(d).wait_recv()
            reduced_t[...] = reduced[...].T

        full = acc[...]
        upper = full.astype(jnp.bfloat16)
        lower = (full - upper.astype(jnp.float32)).astype(jnp.bfloat16)
        left = reduced_t[...]
        joined = dot(left, upper, ((1,), (0,))) + dot(left, lower, ((1,), (0,)))
        for part in range(dp_size):
            span = slice(part * piece, (part + 1) * piece)
            for index in range(3):
                own[head, part // 2, part % 2, index] = joined[
                    span, index * width : (index + 1) * width
                ]
        for to in range(levels):
            pair_out[head, to] = own[head, to, 1 - core].astype(pair_out.dtype)
        pair_copy(head).start()

    def add_pair(head):
        pair_copy(head).wait_recv()
        for to in range(levels):
            total = own[head, to, core] + pair_in[head, to].astype(jnp.float32)
            own[head, to, core] = total
            z_out[head, to] = total.astype(z_out.dtype)
        for d in range(1, levels):
            z_copy(head, d).start()

    def add_levels(head):
        total = own[head, level, core]
        for d in range(1, levels):
            z_copy(head, d).wait_recv()
            total += z_in[head, d - 1].astype(jnp.float32)
        for to in range(ctx_size):
            final_out[head, to] = total[:, to * slab : (to + 1) * slab]
        for d in range(1, ctx_size):
            final_copy(head, d).start()

    @pl.loop(0, heads + 2)
    def _(step):
        @pl.when(step == heads - 1)
        def _():
            add_levels_o()

        @pl.when(step < heads)
        def _():
            compute(step)

        @pl.when(jnp.logical_and(step >= 1, step < heads + 1))
        def _():
            add_pair(step - 1)

        @pl.when(step >= 2)
        def _():
            add_levels(step - 2)

    @pl.loop(0, heads)
    def _(head):
        out_ref[:3, :, columns(me, head)] = final_out[head, me]
        for d in range(1, ctx_size):
            final_copy(head, d).wait()
            owner = lax.rem(me + ctx_size - d, ctx_size)
            out_ref[:3, :, columns(owner, head)] = final_in[head, d - 1]
        pair_copy(head).wait_send()
        for d in range(1, levels):
            z_copy(head, d).wait_send()
        for index in range(count):
            for d in range(1, ctx_size):
                head_copy(head, index, d).wait_send()

    total = final_own_o[me]
    for d in range(1, ctx_size):
        reduced_copy(d).wait_send()
        delta_copy(d).wait_send()
        final_copy_o(d).wait()
        total += final_in_o[d - 1].astype(jnp.float32)
    out_ref[3] = total
    pair_copy_o().wait_send()
    for d in range(1, levels):
        z_copy_o(d).wait_send()


def on_device(
    dp_size,
    ctx_size,
    layer_input,
    queries,
    key_rows,
    value_rows,
    attn_out,
    out_grad,
    layer_grad,
    logsum,
    projector,
):
    rows, features = queries.shape[1:]
    all_heads, tokens = logsum.shape[1:]
    heads = all_heads // ctx_size
    width = features // all_heads
    depth, rank = projector.shape
    levels = dp_size // 2
    piece = rank // dp_size
    slab = piece // ctx_size
    padded = -(-heads // 8) * 8
    low, wide = jnp.bfloat16, jnp.float32
    dma = pltpu.SemaphoreType.DMA
    anywhere = pl.BlockSpec(memory_space=pl.ANY)
    in_vmem = pl.BlockSpec(memory_space=pltpu.VMEM)
    return pl.pallas_call(
        functools.partial(kernel, dp_size, ctx_size),
        out_shape=jax.ShapeDtypeStruct((4, slab, features), wide),
        in_specs=[anywhere] * 7 + [in_vmem, anywhere],
        out_specs=in_vmem,
        scratch_shapes=[
            pltpu.VMEM((4, heads, tokens, width), low),
            pltpu.VMEM((2 * rows, depth), low),
            pltpu.VMEM((depth, rank), low),
            pltpu.VMEM((2 * rows, rank), wide),
            pltpu.VMEM((rows, features), low),
            pltpu.VMEM((rows, features), low),
            pltpu.VMEM((tokens, rank), low),
            pltpu.VMEM((rank, tokens), low),
            pltpu.VMEM((rows, rank), low),
            pltpu.VMEM((ctx_size, padded, rows), wide),
            pltpu.VMEM((ctx_size, padded, rows), wide),
            pltpu.VMEM((padded, tokens), wide),
            pltpu.VMEM((tokens, 3 * width), wide),
            pltpu.VMEM((heads, levels, 2, 3, piece, width), wide),
            pltpu.VMEM((heads, levels, 3, piece, width), low),
            pltpu.VMEM((heads, levels, 3, piece, width), low),
            pltpu.VMEM((heads, levels, 3, piece, width), low),
            pltpu.VMEM((heads, levels - 1, 3, piece, width), low),
            pltpu.VMEM((heads, ctx_size, 3, slab, width), wide),
            pltpu.VMEM((heads, ctx_size - 1, 3, slab, width), wide),
            pltpu.VMEM((levels, 2, piece, features), wide),
            pltpu.VMEM((levels, piece, features), low),
            pltpu.VMEM((levels, piece, features), low),
            pltpu.VMEM((levels, piece, features), low),
            pltpu.VMEM((levels - 1, piece, features), low),
            pltpu.VMEM((ctx_size, slab, features), wide),
            pltpu.VMEM((ctx_size, slab, features), low),
            pltpu.VMEM((ctx_size - 1, slab, features), low),
            dma((5,)),
            dma((heads, 4)),
            dma((heads, 4, ctx_size - 1)),
            dma((heads, 4, ctx_size - 1)),
            dma((ctx_size - 1,)),
            dma((ctx_size - 1,)),
            dma((ctx_size - 1,)),
            dma((ctx_size - 1,)),
            dma((heads,)),
            dma((heads,)),
            dma((heads, levels - 1)),
            dma((heads, levels - 1)),
            dma((heads, ctx_size - 1)),
            dma((heads, ctx_size - 1)),
            dma(()),
            dma(()),
            dma((levels - 1,)),
            dma((levels - 1,)),
            dma((ctx_size - 1,)),
            dma((ctx_size - 1,)),
        ],
        compiler_params=pltpu.CompilerParams(
            collective_id=0, has_side_effects=True, vmem_limit_bytes=56 * 1024 * 1024
        ),
    )(
        layer_input[0],
        queries[0],
        key_rows[0],
        value_rows[0],
        attn_out[0],
        out_grad[0],
        layer_grad[0],
        logsum[0],
        projector,
    )


def solution(mesh):
    rows = P("dp", "ctx", None)
    placed = (rows,) * 7 + (P("dp", None, None), P())
    return jax.shard_map(
        functools.partial(on_device, mesh.shape["dp"], mesh.shape["ctx"]),
        mesh=mesh,
        in_specs=placed,
        out_specs=P(None, ("dp", "ctx"), None),
        check_vma=False,
    )
```

```python
import functools
import math

import jax
import jax.numpy as jnp
from jax import lax
from jax.experimental import pallas as pl
from jax.experimental.pallas import tpu as pltpu
from jax.sharding import PartitionSpec as P

BLOCK = 128
DEPTH = 512
MESH = pl.DeviceIdType.MESH


def dot(left, right, dims):
    return lax.dot_general(left, right, (dims, ((), ())), preferred_element_type=jnp.float32)


def head_products(arrays, head, sums, deltas, acc):
    q_ref, k_ref, v_ref, g_ref = (arrays.at[index, head] for index in range(4))
    tokens, width = q_ref.shape
    scaling = 1.0 / math.sqrt(width)
    row = lax.broadcasted_iota(jnp.int32, (BLOCK, BLOCK), 0)
    col = lax.broadcasted_iota(jnp.int32, (BLOCK, BLOCK), 1)
    causal = row <= col
    for start in range(0, tokens, BLOCK):
        keys = k_ref[start : start + BLOCK]
        values = v_ref[start : start + BLOCK]
        queries = q_ref[start:]
        grads = g_ref[start:]
        scores = dot(keys, queries, ((1,), (1,))) * scaling
        prob = jnp.exp(scores - sums[:, start:])
        diagonal = jnp.where(causal, prob[:, :BLOCK], 0.0)
        if start + BLOCK < tokens:
            prob = jnp.concatenate([diagonal, prob[:, BLOCK:]], axis=1)
        else:
            prob = diagonal
        dprob = dot(values, grads, ((1,), (1,)))
        dscore = prob * (dprob - deltas[:, start:]) * scaling
        score_low = dscore.astype(jnp.bfloat16)
        prob_low = prob.astype(jnp.bfloat16)
        dquery = dot(score_low, keys, ((0,), (0,)))
        if start == 0:
            acc[:, :width] = dquery
        else:
            acc[start:, :width] += dquery
        acc[start : start + BLOCK, width : 2 * width] = dot(score_low, queries, ((1,), (0,)))
        acc[start : start + BLOCK, 2 * width :] = dot(prob_low, grads, ((1,), (0,)))


def kernel(
    dp_size,
    ctx_size,
    layer_input,
    q_hbm,
    k_hbm,
    v_hbm,
    o_hbm,
    g_hbm,
    layer_grad,
    sums_ref,
    projector,
    out_ref,
    arrays,
    rows_in,
    proj,
    proj_acc,
    grad_own,
    out_own,
    reduced,
    reduced_t,
    reduced_grad,
    delta_out,
    delta_in,
    delta_rows,
    acc,
    own,
    sum_out,
    sum_in,
    final_out,
    final_in,
    own_o,
    sum_out_o,
    sum_in_o,
    final_own_o,
    final_out_o,
    final_in_o,
    load_sem,
    local_sem,
    head_send,
    head_recv,
    red_send,
    red_recv,
    delta_send,
    delta_recv,
    sum_send,
    sum_recv,
    final_send,
    final_recv,
    sum_send_o,
    sum_recv_o,
    final_send_o,
    final_recv_o,
):
    me = lax.axis_index("ctx")
    place = lax.axis_index("dp")
    bits = dp_size.bit_length() - 1
    sources = (q_hbm, k_hbm, v_hbm, g_hbm)
    count = len(sources)
    heads = arrays.shape[1]
    rows = q_hbm.shape[0]
    width = arrays.shape[3]
    depth = projector.shape[0]
    piece = own.shape[3]
    slab = final_out.shape[3]
    mine = pl.ds(pl.multiple_of(me * rows, 16), rows)

    def ctx_peer(d):
        return lax.rem(me + d, ctx_size)

    def columns(owner, head):
        return pl.ds(pl.multiple_of((owner * heads + head) * width, width), width)

    def remote(src, dst, send, recv, **where):
        return pltpu.make_async_remote_copy(
            src_ref=src,
            dst_ref=dst,
            send_sem=send,
            recv_sem=recv,
            device_id=where,
            device_id_type=MESH,
        )

    def local_copy(head, index):
        return pltpu.make_async_copy(
            sources[index].at[:, columns(me, head)],
            arrays.at[index, head, mine],
            local_sem.at[head, index],
        )

    def head_copy(head, index, d):
        peer = ctx_peer(d)
        return remote(
            sources[index].at[:, columns(peer, head)],
            arrays.at[index, head, mine],
            head_send.at[head, index, d - 1],
            head_recv.at[head, index, d - 1],
            ctx=peer,
        )

    def reduced_copy(d):
        return remote(
            reduced.at[mine],
            reduced.at[mine],
            red_send.at[d - 1],
            red_recv.at[d - 1],
            ctx=ctx_peer(d),
        )

    def delta_copy(d):
        peer = ctx_peer(d)
        return remote(
            delta_out.at[peer],
            delta_in.at[me],
            delta_send.at[d - 1],
            delta_recv.at[d - 1],
            ctx=peer,
        )

    group_o = (own_o, sum_out_o, sum_in_o, sum_send_o, sum_recv_o)

    def group_of(head):
        return tuple(ref.at[head] for ref in (own, sum_out, sum_in, sum_send, sum_recv))

    def place_bit(stage):
        return lax.rem(place // 2**stage, 2)

    def stage_partner(stage):
        return place + (1 - 2 * place_bit(stage)) * 2**stage

    def stage_copy(group, stage):
        half = dp_size // 2 ** (stage + 1)
        span = pl.ds(dp_size - 2 * half, half)
        return remote(
            group[1].at[span],
            group[2].at[span],
            group[3].at[stage],
            group[4].at[stage],
            dp=stage_partner(stage),
        )

    def stage_blocks(stage, bit):
        half = dp_size // 2 ** (stage + 1)
        first = lax.rem(place, 2**stage) + bit * 2**stage
        return [(first + 2 ** (stage + 1) * j, dp_size - 2 * half + j) for j in range(half)]

    def send_stage(group, stage):
        for block, slot in stage_blocks(stage, 1 - place_bit(stage)):
            group[1][slot] = group[0][block].astype(jnp.bfloat16)
        stage_copy(group, stage).start()

    def add_stage(group, stage):
        stage_copy(group, stage).wait_recv()
        for block, slot in stage_blocks(stage, place_bit(stage)):
            group[0][block] += group[2][slot].astype(jnp.float32)

    def final_copy_o(d):
        peer = ctx_peer(d)
        return remote(
            final_out_o.at[peer],
            final_in_o.at[d - 1],
            final_send_o.at[d - 1],
            final_recv_o.at[d - 1],
            ctx=peer,
        )

    def final_copy(head, d):
        peer = ctx_peer(d)
        return remote(
            final_out.at[head, peer],
            final_in.at[head, d - 1],
            final_send.at[head, d - 1],
            final_recv.at[head, d - 1],
            ctx=peer,
        )

    def start_head(head):
        for index in range(count):
            for d in range(1, ctx_size):
                head_copy(head, index, d).start()
        for index in range(count):
            local_copy(head, index).start()

    loads = (
        pltpu.make_async_copy(g_hbm, grad_own, load_sem.at[0]),
        pltpu.make_async_copy(o_hbm, out_own, load_sem.at[1]),
        pltpu.make_async_copy(projector, proj, load_sem.at[2]),
        pltpu.make_async_copy(layer_input, rows_in.at[:rows], load_sem.at[3]),
        pltpu.make_async_copy(layer_grad, rows_in.at[rows:], load_sem.at[4]),
    )
    for load in loads:
        load.start()
    barrier = pltpu.get_barrier_semaphore()
    for d in range(1, ctx_size):
        pl.semaphore_signal(barrier, inc=1, device_id={"ctx": ctx_peer(d)}, device_id_type=MESH)
    for stage in range(bits):
        peer = stage_partner(stage)
        pl.semaphore_signal(barrier, inc=1, device_id={"dp": peer}, device_id_type=MESH)
    pl.semaphore_wait(barrier, ctx_size - 1 + bits)

    start_head(0)
    for load in loads[:2]:
        load.wait()
    lane = lax.broadcasted_iota(jnp.int32, (rows, BLOCK), 1)
    table = jnp.zeros((rows, BLOCK), jnp.float32)
    for head in range(heads * ctx_size):
        span = slice(head * width, (head + 1) * width)
        product = grad_own[:, span].astype(jnp.float32) * out_own[:, span].astype(jnp.float32)
        table = jnp.where(lane == head, jnp.sum(product, axis=1, keepdims=True), table)
    table = table.T
    delta_out[...] = jnp.zeros_like(delta_out)
    for owner in range(ctx_size):
        delta_out[owner, :heads] = table[owner * heads : (owner + 1) * heads]
    delta_in[me] = delta_out[me]
    for d in range(1, ctx_size):
        delta_copy(d).start()

    for load in loads[2:]:
        load.wait()
    proj_acc[...] = jnp.zeros_like(proj_acc)

    @pl.loop(0, depth // DEPTH)
    def _(step):
        at = pl.ds(pl.multiple_of(step * DEPTH, DEPTH), DEPTH)
        proj_acc[...] += dot(rows_in[:, at], proj[at], ((1,), (0,)))

    reduced[mine] = proj_acc[:rows].astype(jnp.bfloat16)
    for d in range(1, ctx_size):
        reduced_copy(d).start()
    reduced_grad[...] = proj_acc[rows:].astype(jnp.bfloat16)

    @pl.loop(1, heads)
    def _(head):
        start_head(head)

    rgrad_t = reduced_grad[...].T
    for part in range(dp_size):
        span = slice(part * piece, (part + 1) * piece)
        own_o[part] = dot(rgrad_t[span], out_own[...], ((1,), (0,)))
    send_stage(group_o, 0)

    for d in range(1, ctx_size):
        delta_copy(d).wait_recv()
    delta_rows[...] = jnp.concatenate([delta_in[owner] for owner in range(ctx_size)], axis=1)

    def advance_o(stage):
        add_stage(group_o, stage)
        if stage + 1 < bits:
            send_stage(group_o, stage + 1)
        else:
            finish_o()

    def finish_o():
        total = own_o[place]
        for to in range(ctx_size):
            part = total[to * slab : (to + 1) * slab]
            final_own_o[to] = part
            final_out_o[to] = part.astype(final_out_o.dtype)
        for d in range(1, ctx_size):
            final_copy_o(d).start()

    def compute(head):
        for index in range(count):
            local_copy(head, index).wait()
            for d in range(1, ctx_size):
                head_copy(head, index, d).wait_recv()
        sums = sums_ref[pl.ds(me * heads + head, 1), :]
        head_products(arrays, head, sums, delta_rows[pl.ds(head, 1), :], acc)

        @pl.when(head == 0)
        def _():
            for d in range(1, ctx_size):
                reduced_copy(d).wait_recv()
            reduced_t[...] = reduced[...].T

        full = acc[...]
        upper = full.astype(jnp.bfloat16)
        lower = (full - upper.astype(jnp.float32)).astype(jnp.bfloat16)
        left = reduced_t[...]
        joined = dot(left, upper, ((1,), (0,))) + dot(left, lower, ((1,), (0,)))
        for part in range(dp_size):
            span = slice(part * piece, (part + 1) * piece)
            for index in range(3):
                own[head, part, index] = joined[
                    span, index * width : (index + 1) * width
                ]
        send_stage(group_of(head), 0)

    def advance(head, stage):
        add_stage(group_of(head), stage)
        if stage + 1 < bits:
            send_stage(group_of(head), stage + 1)
        else:
            finish(head)

    def finish(head):
        total = own[head, place]
        for to in range(ctx_size):
            final_out[head, to] = total[:, to * slab : (to + 1) * slab]
        for d in range(1, ctx_size):
            final_copy(head, d).start()

    advance_o(0)

    @pl.loop(0, heads + bits - 1)
    def _(step):
        @pl.when(step < heads)
        def _():
            compute(step)
            advance(step, 0)

        for stage in range(1, bits):

            @pl.when(step == stage - 1)
            def _():
                advance_o(stage)

            @pl.when(jnp.logical_and(step >= stage, step < heads + stage))
            def _():
                advance(step - stage, stage)

    @pl.loop(0, heads)
    def _(head):
        out_ref[:3, :, columns(me, head)] = final_out[head, me]
        for d in range(1, ctx_size):
            final_copy(head, d).wait()
            owner = lax.rem(me + ctx_size - d, ctx_size)
            out_ref[:3, :, columns(owner, head)] = final_in[head, d - 1]
        for stage in range(bits):
            stage_copy(group_of(head), stage).wait_send()
        for index in range(count):
            for d in range(1, ctx_size):
                head_copy(head, index, d).wait_send()

    total = final_own_o[me]
    for d in range(1, ctx_size):
        reduced_copy(d).wait_send()
        delta_copy(d).wait_send()
        final_copy_o(d).wait()
        total += final_in_o[d - 1].astype(jnp.float32)
    out_ref[3] = total
    for stage in range(bits):
        stage_copy(group_o, stage).wait_send()


def on_device(
    dp_size,
    ctx_size,
    layer_input,
    queries,
    key_rows,
    value_rows,
    attn_out,
    out_grad,
    layer_grad,
    logsum,
    projector,
):
    rows, features = queries.shape[1:]
    all_heads, tokens = logsum.shape[1:]
    heads = all_heads // ctx_size
    width = features // all_heads
    depth, rank = projector.shape
    bits = dp_size.bit_length() - 1
    piece = rank // dp_size
    slab = piece // ctx_size
    padded = -(-heads // 8) * 8
    low, wide = jnp.bfloat16, jnp.float32
    dma = pltpu.SemaphoreType.DMA
    anywhere = pl.BlockSpec(memory_space=pl.ANY)
    in_vmem = pl.BlockSpec(memory_space=pltpu.VMEM)
    return pl.pallas_call(
        functools.partial(kernel, dp_size, ctx_size),
        out_shape=jax.ShapeDtypeStruct((4, slab, features), wide),
        in_specs=[anywhere] * 7 + [in_vmem, anywhere],
        out_specs=in_vmem,
        scratch_shapes=[
            pltpu.VMEM((4, heads, tokens, width), low),
            pltpu.VMEM((2 * rows, depth), low),
            pltpu.VMEM((depth, rank), low),
            pltpu.VMEM((2 * rows, rank), wide),
            pltpu.VMEM((rows, features), low),
            pltpu.VMEM((rows, features), low),
            pltpu.VMEM((tokens, rank), low),
            pltpu.VMEM((rank, tokens), low),
            pltpu.VMEM((rows, rank), low),
            pltpu.VMEM((ctx_size, padded, rows), wide),
            pltpu.VMEM((ctx_size, padded, rows), wide),
            pltpu.VMEM((padded, tokens), wide),
            pltpu.VMEM((tokens, 3 * width), wide),
            pltpu.VMEM((heads, dp_size, 3, piece, width), wide),
            pltpu.VMEM((heads, dp_size - 1, 3, piece, width), low),
            pltpu.VMEM((heads, dp_size - 1, 3, piece, width), low),
            pltpu.VMEM((heads, ctx_size, 3, slab, width), wide),
            pltpu.VMEM((heads, ctx_size - 1, 3, slab, width), wide),
            pltpu.VMEM((dp_size, piece, features), wide),
            pltpu.VMEM((dp_size - 1, piece, features), low),
            pltpu.VMEM((dp_size - 1, piece, features), low),
            pltpu.VMEM((ctx_size, slab, features), wide),
            pltpu.VMEM((ctx_size, slab, features), low),
            pltpu.VMEM((ctx_size - 1, slab, features), low),
            dma((5,)),
            dma((heads, 4)),
            dma((heads, 4, ctx_size - 1)),
            dma((heads, 4, ctx_size - 1)),
            dma((ctx_size - 1,)),
            dma((ctx_size - 1,)),
            dma((ctx_size - 1,)),
            dma((ctx_size - 1,)),
            dma((heads, bits)),
            dma((heads, bits)),
            dma((heads, ctx_size - 1)),
            dma((heads, ctx_size - 1)),
            dma((bits,)),
            dma((bits,)),
            dma((ctx_size - 1,)),
            dma((ctx_size - 1,)),
        ],
        compiler_params=pltpu.CompilerParams(
            collective_id=0, has_side_effects=True, vmem_limit_bytes=56 * 1024 * 1024
        ),
    )(
        layer_input[0],
        queries[0],
        key_rows[0],
        value_rows[0],
        attn_out[0],
        out_grad[0],
        layer_grad[0],
        logsum[0],
        projector,
    )


def solution(mesh):
    rows = P("dp", "ctx", None)
    placed = (rows,) * 7 + (P("dp", None, None), P())
    return jax.shard_map(
        functools.partial(on_device, mesh.shape["dp"], mesh.shape["ctx"]),
        mesh=mesh,
        in_specs=placed,
        out_specs=P(None, ("dp", "ctx"), None),
        check_vma=False,
    )
```
